512 devices in a mesh: freq: 64 (over z, x_hi, core), space: 8 (over x_lo, y).
Axes of the slice: x: 4 (x_hi: 2, x_lo: 2; x = x_hi * 2 + x_lo), y: 4, z: 16, core: 2. Of those that a mesh axis runs over, the one named last changes fastest.
Arguments:
- series: bfloat16 [2048, 131072], P('freq', 'space')
- starts: int32 [7], replicated, may hold values from 0 to 1536, as said below
- freqs: int32 [64], replicated, may hold values from 0 to 511, as said below
- alpha: int32 [1], replicated, may hold values from 1 to 63
Outputs:
- spectra: bfloat16 [64, 2, 7, 131072], P('freq', None, None, 'space')
- gram: float32 [64, 2, 63, 63], P('freq')
The draws below stay inside these ranges and needn't reach their ends.
Inputs may be any that keep to these rules, and one draw needn't show every extreme that they name: `starts`: increasing; the first is 0, the last 1536; consecutive ones lie 512 / 4 to 384 apart. `freqs`: 64 distinct bins, 0 and 511 among them.
All inputs are finite; a program needn't handle non-finite values.
Results may differ from the reference program's by a relative error of at most 0.005.
Values may be sent and summed in bfloat16 or wider, within the bound.
No kernel may reach another device: no remote copies, remote signals or barrier semaphores. Data moves between devices by JAX's collectives and lax.ppermute only.
A program may use at most 64 MiB of HBM per device.

```python
import math
import jax
import jax.numpy as jnp
from jax import lax

NFFT = 512
NBLK = 7
HALF = 4
C_SP = 16384
SHIFTS = 9
NT = 2048
CELLS = 131072
NFREQ = 64
N_SPACE = 8


def draw_series(key, part):
    keys = jax.random.split(key, 6)
    position = jnp.arange(CELLS, dtype=jnp.float32) / CELLS
    rough = jnp.exp(jax.random.uniform(keys[0], (CELLS,), jnp.float32, -0.1, 0.1))
    amplitude = jnp.sqrt(1.0 + 2.0 * position) * rough / 2.2
    noise = jax.random.normal(keys[1], (NT, CELLS), jnp.float32)
    common_weight = 0.8
    signals = jax.random.normal(keys[2], (3, NT, 1), jnp.float32)
    fields = jax.random.normal(keys[3], (3, 1, CELLS), jnp.float32)
    common = signals[0] * fields[0] + signals[1] * fields[1] + signals[2] * fields[2]
    tone_bins = jax.random.randint(keys[4], (CELLS,), 0, NFFT).astype(jnp.int32)
    tone_start = jax.random.uniform(keys[5], (CELLS,), jnp.float32, -math.pi, math.pi)
    time_index = jnp.arange(NT, dtype=jnp.int32)
    tone_steps = jnp.mod(time_index[:, None] * tone_bins[None, :], NFFT).astype(jnp.float32)
    tone = 2.0 * jnp.cos(tone_steps * (2.0 * math.pi / NFFT) + tone_start[None, :])
    values = amplitude[None, :] * (noise + common_weight * common + tone)
    return jnp.clip(values, -40.0, 40.0).astype(jnp.bfloat16)


def draw_starts(key, part):
    hop_size = NFFT // 2
    jitter = jax.random.randint(key, (NBLK,), -(hop_size // 4), hop_size // 4 + 1)
    nominal = jnp.arange(NBLK, dtype=jnp.int32) * hop_size
    block_index = jnp.arange(NBLK, dtype=jnp.int32)
    inner = (block_index > 0) & (block_index < NBLK - 1)
    return jnp.where(inner, nominal + jitter, nominal).astype(jnp.int32)


def draw_freqs(key, part):
    pick_key = jax.random.fold_in(key, 11)
    order_key = jax.random.fold_in(key, 23)
    inner_bins = jax.random.permutation(pick_key, NFFT - 2)[:NFREQ - 2].astype(jnp.int32) + 1
    ends = jnp.array([0, NFFT - 1], dtype=jnp.int32)
    chosen = jnp.concatenate([ends, inner_bins])
    placing = jax.random.permutation(order_key, NFREQ)
    return chosen[placing].astype(jnp.int32)


def setup_inputs(seed: int = 0) -> dict:
    key_list = jax.random.split(jax.random.key(seed), 5)
    series = draw_series(jax.random.fold_in(key_list[4], 71), 0)
    starts = draw_starts(jax.random.fold_in(key_list[4], 71), 0)
    freqs = draw_freqs(jax.random.fold_in(key_list[4], 71), 0)
    alpha = jax.random.randint(key_list[3], (1,), 1, NFFT // 8).astype(jnp.int32)
    return {"series": series, "starts": starts, "freqs": freqs, "alpha": alpha}


def transform_table(freqs, alpha):
    sample_index = jnp.arange(NFFT, dtype=jnp.int32)
    shift_index = jnp.arange(SHIFTS, dtype=jnp.int32) - HALF
    freq_bins = jnp.mod(freqs[:, None] + shift_index[None, :] * alpha[0], NFFT).astype(jnp.int32)
    phase_steps = jnp.mod(freq_bins[:, :, None] * sample_index[None, None, :], NFFT)
    phase = phase_steps.astype(jnp.float32) * (2.0 * math.pi / NFFT)
    sample_float = sample_index.astype(jnp.float32)
    window_shape = 0.5 - 0.5 * jnp.cos(sample_float * (2.0 * math.pi / NFFT))
    window_scale = window_shape / jnp.sqrt(jnp.sum(window_shape * window_shape))
    real_part = window_scale * jnp.cos(phase)
    imag_part = -(window_scale * jnp.sin(phase))
    return jnp.stack([real_part, imag_part], axis=1).astype(jnp.bfloat16)

def split_quadrants(products, order):
    real_gram = products[..., :order, :order] + products[..., order:, order:]
    imag_gram = products[..., :order, order:] - products[..., order:, :order]
    return jnp.stack([real_gram, imag_gram], axis=-3)

def reference(series, starts, freqs, alpha):
    table = transform_table(freqs, alpha)
    nfreq = freqs.shape[0]
    order = SHIFTS * NBLK
    flat_table = table.reshape(nfreq * 2 * SHIFTS, NFFT).astype(jnp.float32)

    def one_slab(carry, slab_index):
        cell_rows = lax.dynamic_slice_in_dim(series, (slab_index * C_SP).astype(jnp.int32), C_SP, 1)
        blocks = []
        for block in range(NBLK):
            block_rows = lax.dynamic_slice_in_dim(cell_rows, starts[block].astype(jnp.int32), NFFT, 0)
            spec_block = jnp.dot(flat_table, block_rows.astype(jnp.float32), precision=lax.Precision.HIGHEST)
            blocks.append(spec_block.astype(jnp.bfloat16).reshape(nfreq, 2, SHIFTS, C_SP))
        blockspec = jnp.stack(blocks, axis=3)
        stacked = blockspec.reshape(nfreq, 2 * order, C_SP).astype(jnp.float32)
        products = jnp.einsum('jrc,jsc->jrs', stacked, stacked, precision=lax.Precision.HIGHEST)
        return (carry + split_quadrants(products, order), blockspec[:, :, HALF])
    initial = jnp.zeros((nfreq, 2, order, order), jnp.float32)
    summed, own_slabs = lax.scan(one_slab, initial, jnp.arange(N_SPACE, dtype=jnp.int32))
    spectra = jnp.transpose(own_slabs, (1, 2, 3, 0, 4)).reshape(nfreq, 2, NBLK, N_SPACE * C_SP)
    gram = summed / (C_SP * N_SPACE)
    return (spectra, gram)
```

```python
import math

import jax
import jax.numpy as jnp
from jax import lax
from jax.sharding import PartitionSpec as P

NFFT = 512
NBLK = 7
HALF = 4
SHIFTS = 9
ORDER = SHIFTS * NBLK
ENTRIES = 2 * ORDER * ORDER


def transform_table(freqs, alpha):
    sample_index = jnp.arange(NFFT, dtype=jnp.int32)
    shift_index = jnp.arange(SHIFTS, dtype=jnp.int32) - HALF
    freq_bins = jnp.mod(freqs[:, None] + shift_index[None, :] * alpha[0], NFFT)
    phase_steps = jnp.mod(freq_bins[:, :, None] * sample_index[None, None, :], NFFT)
    phase = phase_steps.astype(jnp.float32) * (2.0 * math.pi / NFFT)
    sample_float = sample_index.astype(jnp.float32)
    window_shape = 0.5 - 0.5 * jnp.cos(sample_float * (2.0 * math.pi / NFFT))
    window_scale = window_shape / jnp.sqrt(jnp.sum(window_shape * window_shape))
    real_part = window_scale * jnp.cos(phase)
    imag_part = -(window_scale * jnp.sin(phase))
    return jnp.stack([real_part, imag_part], axis=1).astype(jnp.bfloat16)


def split_quadrants(products, order):
    real_gram = products[..., :order, :order] + products[..., order:, order:]
    imag_gram = products[..., :order, order:] - products[..., order:, :order]
    return jnp.stack([real_gram, imag_gram], axis=-3)


def per_device(series, starts, freqs, alpha):
    slab_cells = series.shape[1]
    n_space = lax.axis_size("space")
    n_freq = freqs.shape[0]
    total_cells = slab_cells * n_space
    cells = slab_cells // n_freq
    piece = -(-ENTRIES // (n_space * 128)) * 128

    rows = lax.all_to_all(series, "freq", split_axis=1, concat_axis=0, tiled=True)
    flat_table = transform_table(freqs, alpha).reshape(n_freq * 2 * SHIFTS, NFFT)
    blocks = []
    for block in range(NBLK):
        block_rows = lax.dynamic_slice_in_dim(rows, starts[block], NFFT, 0)
        spec_block = jnp.dot(flat_table, block_rows, preferred_element_type=jnp.float32)
        blocks.append(spec_block.astype(jnp.bfloat16).reshape(n_freq, 2, SHIFTS, cells))
    blockspec = jnp.stack(blocks, axis=3)
    stacked = blockspec.reshape(n_freq, 2 * ORDER, cells)
    products = jnp.einsum("jrc,jsc->jrs", stacked, stacked, preferred_element_type=jnp.float32)
    partial = split_quadrants(products, ORDER).reshape(n_freq, ENTRIES).astype(jnp.bfloat16)
    partial = jnp.pad(partial, ((0, 0), (0, n_space * piece - ENTRIES)))
    partial = jnp.transpose(partial.reshape(n_freq, n_space, piece), (1, 0, 2))
    gathered = lax.all_to_all(partial, "space", split_axis=0, concat_axis=0, tiled=True)
    slab_sum = jnp.sum(gathered.astype(jnp.float32), axis=0).astype(jnp.bfloat16)

    own = blockspec[:, :, HALF].reshape(n_freq, 2 * NBLK * cells)
    packed = jnp.concatenate([own, slab_sum], axis=1)
    packed = packed.reshape(n_freq, packed.shape[1] // 128, 128)
    received = lax.all_to_all(packed, "freq", split_axis=0, concat_axis=0, tiled=True)
    received = received.reshape(n_freq, -1)
    own = received[:, : 2 * NBLK * cells].reshape(n_freq, 2, NBLK, cells)
    spectra = jnp.transpose(own, (1, 2, 0, 3)).reshape(1, 2, NBLK, slab_cells)
    gram_piece = jnp.sum(received[:, 2 * NBLK * cells :].astype(jnp.float32), axis=0)
    spread = jnp.broadcast_to(gram_piece.reshape(1, piece // 128, 128), (n_space, piece // 128, 128))
    pieces = lax.all_to_all(spread, "space", split_axis=0, concat_axis=0, tiled=True)
    gram = pieces.reshape(-1)[:ENTRIES].reshape(1, 2, ORDER, ORDER) / total_cells
    return (spectra, gram)


def solution(mesh):
    placed = (P("freq", "space"), P(), P(), P())
    return jax.shard_map(
        per_device,
        mesh=mesh,
        in_specs=placed,
        out_specs=(P("freq", None, None, "space"), P("freq", None, None, None)),
        check_vma=False,
    )
```

```python
import functools
import math

import jax
import jax.numpy as jnp
from jax import lax
from jax.experimental import pallas as pl
from jax.experimental.pallas import tpu as pltpu
from jax.sharding import PartitionSpec as P

NFFT = 512
NBLK = 7
HALF = 4
SHIFTS = 9
ORDER = SHIFTS * NBLK
PAD = 64
LANES = 128
ALIGN = 16
PARTS = 2
OWN = PARTS * NBLK


def transform_table(freqs, alpha):
    sample_index = jnp.arange(NFFT, dtype=jnp.int32)
    shift_index = jnp.arange(SHIFTS, dtype=jnp.int32) - HALF
    freq_bins = jnp.mod(freqs[None, :] + shift_index[:, None] * alpha[0], NFFT)
    phase_steps = jnp.mod(freq_bins[:, :, None] * sample_index[None, None, :], NFFT)
    phase = phase_steps.astype(jnp.float32) * (2.0 * math.pi / NFFT)
    sample_float = sample_index.astype(jnp.float32)
    window_shape = 0.5 - 0.5 * jnp.cos(sample_float * (2.0 * math.pi / NFFT))
    window_scale = window_shape / jnp.sqrt(jnp.sum(window_shape * window_shape))
    real_part = window_scale * jnp.cos(phase)
    imag_part = -(window_scale * jnp.sin(phase))
    return jnp.stack([real_part, imag_part], axis=0).astype(jnp.bfloat16)


def middle_kernel(n_freq, halves, piece_rows, starts_ref, rows_ref, table_ref, own_ref, gram_ref,
                  spec32, own32, gram32):
    span = 2 * PAD
    samples = rows_ref.shape[0]
    zero = jnp.zeros((n_freq, LANES), jnp.float32)
    for half in range(halves):
        for part in range(PARTS):
            spec32[half, pl.ds(part * PAD + ORDER, n_freq, stride=span), :] = zero
    for block in range(NBLK):
        start = starts_ref[block]
        aligned = jnp.minimum(start // ALIGN * ALIGN, samples - NFFT - ALIGN)
        window = rows_ref[pl.ds(pl.multiple_of(aligned, ALIGN), NFFT + ALIGN), :].astype(jnp.float32)
        shifted = pltpu.roll(window, lax.rem(NFFT + ALIGN - (start - aligned), NFFT + ALIGN), 0)
        block_rows = shifted[:NFFT].astype(jnp.bfloat16)
        spec = jnp.dot(table_ref[...], block_rows, preferred_element_type=jnp.float32)
        for part in range(PARTS):
            for shift in range(SHIFTS):
                base = (part * SHIFTS + shift) * n_freq
                row = part * PAD + shift * NBLK + block
                for half in range(halves):
                    values = spec[base : base + n_freq, half * LANES : (half + 1) * LANES]
                    spec32[half, pl.ds(row, n_freq, stride=span), :] = values
                    if shift == HALF:
                        own_row = (part * NBLK + block) * halves + half
                        own32[pl.ds(own_row, n_freq, stride=OWN * halves), :] = values
    own_ref[...] = own32[...].astype(jnp.bfloat16)

    row_index = lax.broadcasted_iota(jnp.int32, (PAD, LANES), 0)
    lane_index = lax.broadcasted_iota(jnp.int32, (PAD, LANES), 1)
    low = lane_index < PAD
    column = jnp.where(low, lane_index, lane_index - PAD)
    keep = (row_index <= column) == low
    sign = jnp.where(low, 1.0, -1.0)
    low_half = low[: PAD // 2]

    def one_frequency(j, carry):
        first = pl.multiple_of(j * span, span)
        stacked = jnp.concatenate(
            [spec32[half, pl.ds(first, span), :] for half in range(halves)], axis=1
        ).astype(jnp.bfloat16)
        products = lax.dot_general(
            stacked, stacked, (((1,), (1,)), ((), ())), preferred_element_type=jnp.float32
        )
        both = products[:PAD] + sign * pltpu.roll(products[PAD:], PAD, 1)
        merged = jnp.where(keep, both, pltpu.roll(both, PAD, 1))
        packed = jnp.where(low_half, merged[: PAD // 2], merged[PAD // 2 :])
        n_piece = (PAD // 2) // piece_rows
        for p in range(n_piece):
            target = p * n_freq * piece_rows + j * piece_rows
            gram32[pl.ds(target, piece_rows), :] = packed[p * piece_rows : (p + 1) * piece_rows]
        return carry

    lax.fori_loop(0, n_freq, one_frequency, 0)
    gram_ref[...] = gram32[...].astype(jnp.bfloat16)


def transform_and_gram(starts, rows, table, n_freq, piece_rows):
    samples, cells = rows.shape
    halves = cells // LANES
    own_rows = n_freq * OWN * halves
    gram_rows = n_freq * (PAD // 2)
    vmem = pl.BlockSpec(memory_space=pltpu.VMEM)
    flops = 2 * NBLK * table.shape[0] * NFFT * cells + 2 * n_freq * (2 * PAD) ** 2 * cells
    return pl.pallas_call(
        functools.partial(middle_kernel, n_freq, halves, piece_rows),
        out_shape=(
            jax.ShapeDtypeStruct((own_rows, LANES), jnp.bfloat16),
            jax.ShapeDtypeStruct((gram_rows, LANES), jnp.bfloat16),
        ),
        in_specs=[pl.BlockSpec(memory_space=pltpu.SMEM), vmem, vmem],
        out_specs=(vmem, vmem),
        scratch_shapes=[
            pltpu.VMEM((halves, n_freq * 2 * PAD, LANES), jnp.float32),
            pltpu.VMEM((own_rows, LANES), jnp.float32),
            pltpu.VMEM((gram_rows, LANES), jnp.float32),
        ],
        cost_estimate=pl.CostEstimate(flops=flops, bytes_accessed=4 << 20, transcendentals=0),
        name="transform_and_gram",
    )(starts, rows, table)


def unpack_gram(packed):
    square = jnp.concatenate([packed[:, :PAD], packed[:, PAD:]], axis=0)[:ORDER, :ORDER]
    upper = jnp.arange(ORDER)[:, None] <= jnp.arange(ORDER)[None, :]
    diagonal = jnp.arange(ORDER)[:, None] == jnp.arange(ORDER)[None, :]
    real_gram = jnp.where(upper, square, square.T)
    imag_gram = jnp.where(upper, jnp.where(diagonal, 0.0, -square.T), square)
    return jnp.stack([real_gram, imag_gram], axis=0)


def per_device(series, starts, freqs, alpha):
    slab_cells = series.shape[1]
    n_space = lax.axis_size("space")
    n_freq = freqs.shape[0]
    total_cells = slab_cells * n_space
    cells = slab_cells // n_freq
    halves = cells // LANES
    piece_rows = (PAD // 2) // n_space

    rows = lax.all_to_all(series, "freq", split_axis=1, concat_axis=0, tiled=True)
    table = transform_table(freqs, alpha).reshape(PARTS * SHIFTS * n_freq, NFFT)
    own, partial = transform_and_gram(starts, rows, table, n_freq, piece_rows)

    partial = partial.reshape(n_space, n_freq * piece_rows, LANES)
    gathered = lax.all_to_all(partial, "space", split_axis=0, concat_axis=0, tiled=True)
    slab_sum = jnp.sum(gathered.astype(jnp.float32), axis=0).astype(jnp.bfloat16)

    packed = jnp.concatenate(
        [own.reshape(n_freq, OWN * halves, LANES), slab_sum.reshape(n_freq, piece_rows, LANES)], axis=1
    )
    received = lax.all_to_all(packed, "freq", split_axis=0, concat_axis=0, tiled=True)
    own = received[:, : OWN * halves].reshape(n_freq, PARTS, NBLK, cells)
    spectra = jnp.transpose(own, (1, 2, 0, 3)).reshape(1, PARTS, NBLK, slab_cells)
    gram_piece = jnp.sum(received[:, OWN * halves :].astype(jnp.float32), axis=0)
    spread = jnp.broadcast_to(gram_piece[None], (n_space, piece_rows, LANES))
    pieces = lax.all_to_all(spread, "space", split_axis=0, concat_axis=0, tiled=True)
    gram = unpack_gram(pieces.reshape(PAD // 2, LANES) / total_cells)[None]
    return (spectra, gram)


def solution(mesh):
    placed = (P("freq", "space"), P(), P(), P())
    return jax.shard_map(
        per_device,
        mesh=mesh,
        in_specs=placed,
        out_specs=(P("freq", None, None, "space"), P("freq", None, None, None)),
        check_vma=False,
    )
```

```python
import functools
import math

import jax
import jax.numpy as jnp
from jax import lax
from jax.experimental import pallas as pl
from jax.experimental.pallas import tpu as pltpu
from jax.sharding import PartitionSpec as P

NFFT = 512
NBLK = 7
HALF = 4
SHIFTS = 9
ORDER = SHIFTS * NBLK
PAD = 64
LANES = 128
SPREAD = 2
SPAN = 136
PARTS = 2
OWN = PARTS * NBLK


def transform_table(freqs, alpha):
    sample_index = jnp.arange(NFFT, dtype=jnp.int32)
    shift_index = jnp.arange(SHIFTS, dtype=jnp.int32) - HALF
    freq_bins = jnp.mod(freqs[None, :] + shift_index[:, None] * alpha[0], NFFT)
    phase_steps = jnp.mod(freq_bins[:, :, None] * sample_index[None, None, :], NFFT)
    phase = phase_steps.astype(jnp.float32) * (2.0 * math.pi / NFFT)
    sample_float = sample_index.astype(jnp.float32)
    window_shape = 0.5 - 0.5 * jnp.cos(sample_float * (2.0 * math.pi / NFFT))
    window_scale = window_shape / jnp.sqrt(jnp.sum(window_shape * window_shape))
    real_part = window_scale * jnp.cos(phase)
    imag_part = -(window_scale * jnp.sin(phase))
    return jnp.stack([real_part, imag_part], axis=0).astype(jnp.bfloat16)


def middle_kernel(n_freq, halves, piece_rows, starts_ref, rows_ref, table_ref, own_ref, gram_ref,
                  rows32, spec32, own32, gram32):
    samples = rows_ref.shape[0]
    for half in range(halves):
        lanes = slice(half * LANES, (half + 1) * LANES)
        rows32[half, pl.ds(0, samples, stride=SPREAD), :] = rows_ref[:, lanes].astype(jnp.float32)
        for part in range(PARTS):
            zero = jnp.zeros((n_freq, LANES), jnp.float32)
            spec32[half, pl.ds(part * PAD + ORDER, n_freq, stride=SPAN), :] = zero

    def one_block(block, carry):
        first = starts_ref[block] * SPREAD
        block_rows = jnp.concatenate(
            [rows32[half, pl.ds(first, NFFT, stride=SPREAD), :] for half in range(halves)], axis=1
        ).astype(jnp.bfloat16)
        spec = jnp.dot(table_ref[...], block_rows, preferred_element_type=jnp.float32)
        for part in range(PARTS):
            for shift in range(SHIFTS):
                base = (part * SHIFTS + shift) * n_freq
                row = part * PAD + shift * NBLK + block
                for half in range(halves):
                    values = spec[base : base + n_freq, half * LANES : (half + 1) * LANES]
                    spec32[half, pl.ds(row, n_freq, stride=SPAN), :] = values
                    if shift == HALF:
                        own_row = (part * NBLK + block) * halves + half
                        own32[pl.ds(own_row, n_freq, stride=OWN * halves), :] = values
        return carry

    lax.fori_loop(0, NBLK, one_block, 0, unroll=True)
    own_ref[...] = own32[...].astype(jnp.bfloat16)

    row_index = lax.broadcasted_iota(jnp.int32, (PAD, LANES), 0)
    lane_index = lax.broadcasted_iota(jnp.int32, (PAD, LANES), 1)
    low = lane_index < PAD
    column = jnp.where(low, lane_index, lane_index - PAD)
    keep = (row_index <= column) == low
    sign = jnp.where(low, 1.0, -1.0)
    low_half = low[: PAD // 2]

    def one_frequency(j, carry):
        first = pl.multiple_of(j * SPAN, 8)
        stacked = jnp.concatenate(
            [spec32[half, pl.ds(first, 2 * PAD), :] for half in range(halves)], axis=1
        ).astype(jnp.bfloat16)
        products = lax.dot_general(
            stacked, stacked, (((1,), (1,)), ((), ())), preferred_element_type=jnp.float32
        )
        both = products[:PAD] + sign * pltpu.roll(products[PAD:], PAD, 1)
        merged = jnp.where(keep, both, pltpu.roll(both, PAD, 1))
        packed = jnp.where(low_half, merged[: PAD // 2], merged[PAD // 2 :])
        for p in range(PAD // 2 // piece_rows):
            target = p * n_freq * piece_rows + j * piece_rows
            gram32[pl.ds(target, piece_rows), :] = packed[p * piece_rows : (p + 1) * piece_rows]
        return carry

    lax.fori_loop(0, n_freq, one_frequency, 0, unroll=8)
    gram_ref[...] = gram32[...].astype(jnp.bfloat16)


def transform_and_gram(starts, rows, table, n_freq, piece_rows):
    samples, cells = rows.shape
    halves = cells // LANES
    own_rows = n_freq * OWN * halves
    gram_rows = n_freq * (PAD // 2)
    vmem = pl.BlockSpec(memory_space=pltpu.VMEM)
    flops = 2 * NBLK * table.shape[0] * NFFT * cells + 2 * n_freq * (2 * PAD) ** 2 * cells
    return pl.pallas_call(
        functools.partial(middle_kernel, n_freq, halves, piece_rows),
        out_shape=(
            jax.ShapeDtypeStruct((own_rows, LANES), jnp.bfloat16),
            jax.ShapeDtypeStruct((gram_rows, LANES), jnp.bfloat16),
        ),
        in_specs=[pl.BlockSpec(memory_space=pltpu.SMEM), vmem, vmem],
        out_specs=(vmem, vmem),
        scratch_shapes=[
            pltpu.VMEM((halves, samples * SPREAD, LANES), jnp.float32),
            pltpu.VMEM((halves, n_freq * SPAN, LANES), jnp.float32),
            pltpu.VMEM((own_rows, LANES), jnp.float32),
            pltpu.VMEM((gram_rows, LANES), jnp.float32),
        ],
        cost_estimate=pl.CostEstimate(flops=flops, bytes_accessed=4 << 20, transcendentals=0),
        compiler_params=pltpu.CompilerParams(vmem_limit_bytes=28 << 20),
        name="transform_and_gram",
    )(starts, rows, table)


def unpack_gram(packed):
    square = jnp.concatenate([packed[:, :PAD], packed[:, PAD:]], axis=0)[:ORDER, :ORDER]
    upper = jnp.arange(ORDER)[:, None] <= jnp.arange(ORDER)[None, :]
    diagonal = jnp.arange(ORDER)[:, None] == jnp.arange(ORDER)[None, :]
    real_gram = jnp.where(upper, square, square.T)
    imag_gram = jnp.where(upper, jnp.where(diagonal, 0.0, -square.T), square)
    return jnp.stack([real_gram, imag_gram], axis=0)


def per_device(series, starts, freqs, alpha):
    slab_cells = series.shape[1]
    n_space = lax.axis_size("space")
    n_freq = freqs.shape[0]
    total_cells = slab_cells * n_space
    cells = slab_cells // n_freq
    halves = cells // LANES
    piece_rows = (PAD // 2) // n_space

    rows = lax.all_to_all(series, "freq", split_axis=1, concat_axis=0, tiled=True)
    table = transform_table(freqs, alpha).reshape(PARTS * SHIFTS * n_freq, NFFT)
    own, partial = transform_and_gram(starts, rows, table, n_freq, piece_rows)

    partial = partial.reshape(n_space, n_freq * piece_rows, LANES)
    gathered = lax.all_to_all(partial, "space", split_axis=0, concat_axis=0, tiled=True)
    slab_sum = jnp.sum(gathered.astype(jnp.float32), axis=0).astype(jnp.bfloat16)

    packed = jnp.concatenate(
        [own.reshape(n_freq, OWN * halves, LANES), slab_sum.reshape(n_freq, piece_rows, LANES)], axis=1
    )
    received = lax.all_to_all(packed, "freq", split_axis=0, concat_axis=0, tiled=True)
    own = received[:, : OWN * halves].reshape(n_freq, PARTS, NBLK, cells)
    spectra = jnp.transpose(own, (1, 2, 0, 3)).reshape(1, PARTS, NBLK, slab_cells)
    gram_piece = jnp.sum(received[:, OWN * halves :].astype(jnp.float32), axis=0)
    spread = jnp.broadcast_to(gram_piece[None], (n_space, piece_rows, LANES))
    pieces = lax.all_to_all(spread, "space", split_axis=0, concat_axis=0, tiled=True)
    gram = unpack_gram(pieces.reshape(PAD // 2, LANES) / total_cells)[None]
    return (spectra, gram)


def solution(mesh):
    placed = (P("freq", "space"), P(), P(), P())
    return jax.shard_map(
        per_device,
        mesh=mesh,
        in_specs=placed,
        out_specs=(P("freq", None, None, "space"), P("freq", None, None, None)),
        check_vma=False,
    )
```

```python
import functools
import math

import jax
import jax.numpy as jnp
from jax import lax
from jax.experimental import pallas as pl
from jax.experimental.pallas import tpu as pltpu
from jax.sharding import PartitionSpec as P

NFFT = 512
NBLK = 7
HALF = 4
SHIFTS = 9
ORDER = SHIFTS * NBLK
PAD = 64
LANES = 128
SPREAD = 2
SPAN = 136
PARTS = 2
OWN = PARTS * NBLK


def transform_table(freqs, alpha):
    sample_index = jnp.arange(NFFT, dtype=jnp.int32)
    shift_index = jnp.arange(SHIFTS, dtype=jnp.int32) - HALF
    freq_bins = jnp.mod(freqs[None, :] + shift_index[:, None] * alpha[0], NFFT)
    phase_steps = jnp.mod(freq_bins[:, :, None] * sample_index[None, None, :], NFFT)
    phase = phase_steps.astype(jnp.float32) * (2.0 * math.pi / NFFT)
    sample_float = sample_index.astype(jnp.float32)
    window_shape = 0.5 - 0.5 * jnp.cos(sample_float * (2.0 * math.pi / NFFT))
    window_scale = window_shape / jnp.sqrt(jnp.sum(window_shape * window_shape))
    real_part = window_scale * jnp.cos(phase)
    imag_part = -(window_scale * jnp.sin(phase))
    return jnp.stack([real_part, imag_part], axis=0).astype(jnp.bfloat16)


def middle_kernel(n_out, scalars_ref, mine_ref, other_ref, table_ref, out_ref, rows32, spec32, out32):
    quarters, spread_rows, _ = rows32.shape
    message = out_ref.shape[0] // n_out
    own_rows = OWN * quarters
    run = spread_rows // SPREAD // (2 * n_out)
    core = scalars_ref[NBLK]
    for quarter in range(quarters):
        lanes = slice(quarter * LANES, (quarter + 1) * LANES)
        for source in range(n_out):
            taken = slice(source * run, (source + 1) * run)
            for ref, side in ((mine_ref, core), (other_ref, 1 - core)):
                first = SPREAD * run * (2 * source + side)
                rows32[quarter, pl.ds(first, run, stride=SPREAD), :] = ref[taken, lanes].astype(jnp.float32)
        for part in range(PARTS):
            zero = jnp.zeros((n_out, LANES), jnp.float32)
            spec32[quarter, pl.ds(part * PAD + ORDER, n_out, stride=SPAN), :] = zero

    for block in range(NBLK):
        first = scalars_ref[block] * SPREAD
        block_rows = jnp.concatenate(
            [rows32[quarter, pl.ds(first, NFFT, stride=SPREAD), :] for quarter in range(quarters)], axis=1
        ).astype(jnp.bfloat16)
        spec = jnp.dot(table_ref[...], block_rows, preferred_element_type=jnp.float32)
        for part in range(PARTS):
            for shift in range(SHIFTS):
                base = (part * SHIFTS + shift) * n_out
                row = part * PAD + shift * NBLK + block
                for quarter in range(quarters):
                    values = spec[base : base + n_out, quarter * LANES : (quarter + 1) * LANES]
                    spec32[quarter, pl.ds(row, n_out, stride=SPAN), :] = values
                    if shift == HALF:
                        own_row = (part * NBLK + block) * quarters + quarter
                        out32[pl.ds(own_row, n_out, stride=message), :] = values

    row_index = lax.broadcasted_iota(jnp.int32, (PAD, LANES), 0)
    lane_index = lax.broadcasted_iota(jnp.int32, (PAD, LANES), 1)
    low = lane_index < PAD
    column = jnp.where(low, lane_index, lane_index - PAD)
    keep = (row_index <= column) == low
    sign = jnp.where(low, 1.0, -1.0)
    low_half = low[: PAD // 2]

    def one_frequency(j, carry):
        first = pl.multiple_of(j * SPAN, 8)
        stacked = jnp.concatenate(
            [spec32[quarter, pl.ds(first, 2 * PAD), :] for quarter in range(quarters)], axis=1
        ).astype(jnp.bfloat16)
        products = lax.dot_general(
            stacked, stacked, (((1,), (1,)), ((), ())), preferred_element_type=jnp.float32
        )
        both = products[:PAD] + sign * pltpu.roll(products[PAD:], PAD, 1)
        merged = jnp.where(keep, both, pltpu.roll(both, PAD, 1))
        packed = jnp.where(low_half, merged[: PAD // 2], merged[PAD // 2 :])
        out32[pl.ds(pl.multiple_of(j * message + own_rows, 8), PAD // 2), :] = packed
        return carry

    lax.fori_loop(0, n_out, one_frequency, 0, unroll=8)
    out_ref[...] = out32[...].astype(jnp.bfloat16)


def transform_and_gram(scalars, mine, other, table, n_out):
    run_rows, cells = mine.shape
    quarters = cells // LANES
    out_rows = n_out * (OWN * quarters + PAD // 2)
    vmem = pl.BlockSpec(memory_space=pltpu.VMEM)
    flops = 2 * NBLK * table.shape[0] * NFFT * cells + 2 * n_out * (2 * PAD) ** 2 * cells
    return pl.pallas_call(
        functools.partial(middle_kernel, n_out),
        out_shape=jax.ShapeDtypeStruct((out_rows, LANES), jnp.bfloat16),
        in_specs=[pl.BlockSpec(memory_space=pltpu.SMEM), vmem, vmem, vmem],
        out_specs=vmem,
        scratch_shapes=[
            pltpu.VMEM((quarters, 2 * run_rows * SPREAD, LANES), jnp.float32),
            pltpu.VMEM((quarters, n_out * SPAN, LANES), jnp.float32),
            pltpu.VMEM((out_rows, LANES), jnp.float32),
        ],
        cost_estimate=pl.CostEstimate(flops=flops, bytes_accessed=4 << 20, transcendentals=0),
        compiler_params=pltpu.CompilerParams(vmem_limit_bytes=32 << 20),
        name="transform_and_gram",
    )(scalars, mine, other, table)


def unpack_gram(packed):
    square = jnp.concatenate([packed[:, :PAD], packed[:, PAD:]], axis=0)[:ORDER, :ORDER]
    upper = jnp.arange(ORDER)[:, None] <= jnp.arange(ORDER)[None, :]
    diagonal = jnp.arange(ORDER)[:, None] == jnp.arange(ORDER)[None, :]
    real_gram = jnp.where(upper, square, square.T)
    imag_gram = jnp.where(upper, jnp.where(diagonal, 0.0, -square.T), square)
    return jnp.stack([real_gram, imag_gram], axis=0)


def per_device(series, starts, freqs, alpha):
    slab_cells = series.shape[1]
    n_space = lax.axis_size("space")
    n_freq = freqs.shape[0]
    n_out = n_freq // 2
    total_cells = slab_cells * n_space
    cells = slab_cells // n_out
    quarters = cells // LANES
    core = lax.rem(lax.axis_index("freq"), 2)
    same_core = [[2 * chip + side for chip in range(n_out)] for side in range(2)]

    mine = lax.all_to_all(
        series, "freq", split_axis=1, concat_axis=0, tiled=True, axis_index_groups=same_core
    )
    own_freqs = jnp.where(core == 0, freqs[0::2], freqs[1::2])
    table = transform_table(own_freqs, alpha).reshape(PARTS * SHIFTS * n_out, NFFT)
    scalars = jnp.concatenate([starts, core[None].astype(starts.dtype)])
    mine, table, scalars = lax.optimization_barrier((mine, table, scalars))
    other = lax.ppermute(mine, "freq", [(index, index ^ 1) for index in range(n_freq)])
    message = transform_and_gram(scalars, mine, other, table, n_out).reshape(n_out, -1, LANES)
    received = lax.all_to_all(
        message, "freq", split_axis=0, concat_axis=0, tiled=True, axis_index_groups=same_core
    )
    own = received[:, : OWN * quarters].reshape(n_out, PARTS, NBLK, cells)
    spectra = jnp.transpose(own, (1, 2, 0, 3)).reshape(1, PARTS, NBLK, slab_cells)
    slab_gram = jnp.sum(received[:, OWN * quarters :].astype(jnp.float32), axis=0)
    spread = jnp.broadcast_to(slab_gram[None], (n_space, PAD // 2, LANES))
    slabs = lax.all_to_all(spread, "space", split_axis=0, concat_axis=0, tiled=True)
    gram = unpack_gram(jnp.sum(slabs, axis=0) / total_cells)[None]
    return (spectra, gram)


def solution(mesh):
    placed = (P("freq", "space"), P(), P(), P())
    return jax.shard_map(
        per_device,
        mesh=mesh,
        in_specs=placed,
        out_specs=(P("freq", None, None, "space"), P("freq", None, None, None)),
        check_vma=False,
    )
```

```python
import functools
import math

import jax
import jax.numpy as jnp
from jax import lax
from jax.experimental import pallas as pl
from jax.experimental.pallas import tpu as pltpu
from jax.sharding import PartitionSpec as P

NFFT = 512
NBLK = 7
HALF = 4
SHIFTS = 9
ORDER = SHIFTS * NBLK
PAD = 64
LANES = 128
SPREAD = 2
SPAN = 136
PARTS = 2
OWN = PARTS * NBLK


def transform_table(freqs, alpha):
    sample_index = jnp.arange(NFFT, dtype=jnp.int32)
    shift_index = jnp.arange(SHIFTS, dtype=jnp.int32) - HALF
    freq_bins = jnp.mod(freqs[None, :] + shift_index[:, None] * alpha[0], NFFT)
    phase_steps = jnp.mod(freq_bins[:, :, None] * sample_index[None, None, :], NFFT)
    phase = phase_steps.astype(jnp.float32) * (2.0 * math.pi / NFFT)
    sample_float = sample_index.astype(jnp.float32)
    window_shape = 0.5 - 0.5 * jnp.cos(sample_float * (2.0 * math.pi / NFFT))
    window_scale = window_shape / jnp.sqrt(jnp.sum(window_shape * window_shape))
    real_part = window_scale * jnp.cos(phase)
    imag_part = -(window_scale * jnp.sin(phase))
    return jnp.stack([real_part, imag_part], axis=0).astype(jnp.bfloat16)


def middle_kernel(n_out, scalars_ref, mine_ref, other_ref, table_ref, out_ref, rows32, spec32, out32):
    quarters, spread_rows, _ = rows32.shape
    message = out_ref.shape[0] // n_out
    own_rows = OWN * quarters
    run = spread_rows // SPREAD // (2 * n_out)
    core = scalars_ref[NBLK]
    for quarter in range(quarters):
        lanes = slice(quarter * LANES, (quarter + 1) * LANES)
        for source in range(n_out):
            taken = slice(source * run, (source + 1) * run)
            for ref, side in ((mine_ref, core), (other_ref, 1 - core)):
                first = SPREAD * run * (2 * source + side)
                rows32[quarter, pl.ds(first, run, stride=SPREAD), :] = ref[taken, lanes].astype(jnp.float32)
        for part in range(PARTS):
            zero = jnp.zeros((n_out, LANES), jnp.float32)
            spec32[quarter, pl.ds(part * PAD + ORDER, n_out, stride=SPAN), :] = zero

    for block in range(NBLK):
        first = scalars_ref[block] * SPREAD
        block_rows = jnp.concatenate(
            [rows32[quarter, pl.ds(first, NFFT, stride=SPREAD), :] for quarter in range(quarters)], axis=1
        ).astype(jnp.bfloat16)
        spec = jnp.dot(table_ref[...], block_rows, preferred_element_type=jnp.float32)
        for part in range(PARTS):
            for shift in range(SHIFTS):
                base = (part * SHIFTS + shift) * n_out
                row = part * PAD + shift * NBLK + block
                for quarter in range(quarters):
                    values = spec[base : base + n_out, quarter * LANES : (quarter + 1) * LANES]
                    spec32[quarter, pl.ds(row, n_out, stride=SPAN), :] = values
                    if shift == HALF:
                        own_row = (part * NBLK + block) * quarters + quarter
                        out32[pl.ds(own_row, n_out, stride=message), :] = values

    row_index = lax.broadcasted_iota(jnp.int32, (PAD, LANES), 0)
    lane_index = lax.broadcasted_iota(jnp.int32, (PAD, LANES), 1)
    low = lane_index < PAD
    column = jnp.where(low, lane_index, lane_index - PAD)
    keep = (row_index <= column) == low
    sign = jnp.where(low, 1.0, -1.0)
    low_half = low[: PAD // 2]

    def one_frequency(j, carry):
        first = pl.multiple_of(j * SPAN, 8)
        stacked = jnp.concatenate(
            [spec32[quarter, pl.ds(first, 2 * PAD), :] for quarter in range(quarters)], axis=1
        ).astype(jnp.bfloat16)
        products = lax.dot_general(
            stacked, stacked, (((1,), (1,)), ((), ())), preferred_element_type=jnp.float32
        )
        both = products[:PAD] + sign * pltpu.roll(products[PAD:], PAD, 1)
        merged = jnp.where(keep, both, pltpu.roll(both, PAD, 1))
        packed = jnp.where(low_half, merged[: PAD // 2], merged[PAD // 2 :])
        out32[pl.ds(pl.multiple_of(j * message + own_rows, 8), PAD // 2), :] = packed
        return carry

    lax.fori_loop(0, n_out, one_frequency, 0, unroll=8)
    out_ref[...] = out32[...].astype(jnp.bfloat16)


def transform_and_gram(scalars, mine, other, table, n_out):
    run_rows, cells = mine.shape
    quarters = cells // LANES
    out_rows = n_out * (OWN * quarters + PAD // 2)
    vmem = pl.BlockSpec(memory_space=pltpu.VMEM)
    flops = 2 * NBLK * table.shape[0] * NFFT * cells + 2 * n_out * (2 * PAD) ** 2 * cells
    return pl.pallas_call(
        functools.partial(middle_kernel, n_out),
        out_shape=jax.ShapeDtypeStruct((out_rows, LANES), jnp.bfloat16),
        in_specs=[pl.BlockSpec(memory_space=pltpu.SMEM), vmem, vmem, vmem],
        out_specs=vmem,
        scratch_shapes=[
            pltpu.VMEM((quarters, 2 * run_rows * SPREAD, LANES), jnp.float32),
            pltpu.VMEM((quarters, n_out * SPAN, LANES), jnp.float32),
            pltpu.VMEM((out_rows, LANES), jnp.float32),
        ],
        cost_estimate=pl.CostEstimate(flops=flops, bytes_accessed=4 << 20, transcendentals=0),
        compiler_params=pltpu.CompilerParams(vmem_limit_bytes=32 << 20),
        name="transform_and_gram",
    )(scalars, mine, other, table)


def unpack_gram(packed):
    square = jnp.concatenate([packed[:, :PAD], packed[:, PAD:]], axis=0)[:ORDER, :ORDER]
    upper = jnp.arange(ORDER)[:, None] <= jnp.arange(ORDER)[None, :]
    diagonal = jnp.arange(ORDER)[:, None] == jnp.arange(ORDER)[None, :]
    real_gram = jnp.where(upper, square, square.T)
    imag_gram = jnp.where(upper, jnp.where(diagonal, 0.0, -square.T), square)
    return jnp.stack([real_gram, imag_gram], axis=0)


def per_device(series, starts, freqs, alpha):
    slab_cells = series.shape[1]
    n_space = lax.axis_size("space")
    n_freq = freqs.shape[0]
    n_out = n_freq // 2
    total_cells = slab_cells * n_space
    cells = slab_cells // n_out
    quarters = cells // LANES
    core = lax.rem(lax.axis_index("freq"), 2)
    same_core = [[2 * chip + side for chip in range(n_out)] for side in range(2)]

    mine = lax.all_to_all(
        series, "freq", split_axis=1, concat_axis=0, tiled=True, axis_index_groups=same_core
    )
    own_freqs = jnp.where(core == 0, freqs[0::2], freqs[1::2])
    table = transform_table(own_freqs, alpha).reshape(PARTS * SHIFTS * n_out, NFFT)
    scalars = jnp.concatenate([starts, core[None].astype(starts.dtype)])
    mine, table, scalars = lax.optimization_barrier((mine, table, scalars))
    other = lax.ppermute(mine, "freq", [(index, index ^ 1) for index in range(n_freq)])
    message = transform_and_gram(scalars, mine, other, table, n_out).reshape(n_out, -1, LANES)
    received = lax.all_to_all(
        message, "freq", split_axis=0, concat_axis=0, tiled=True, axis_index_groups=same_core
    )
    own = received[:, : OWN * quarters].reshape(n_out, PARTS, NBLK, cells)
    spectra = jnp.transpose(own, (1, 2, 0, 3)).reshape(1, PARTS, NBLK, slab_cells)
    slab_gram = jnp.sum(received[:, OWN * quarters :].astype(jnp.float32), axis=0)
    spread = jnp.broadcast_to(slab_gram[None], (n_space, PAD // 2, LANES))
    spread, spectra = lax.optimization_barrier((spread, spectra))
    slabs = lax.all_to_all(spread, "space", split_axis=0, concat_axis=0, tiled=True)
    gram = unpack_gram(jnp.sum(slabs, axis=0) / total_cells)[None]
    return (spectra, gram)


def solution(mesh):
    placed = (P("freq", "space"), P(), P(), P())
    return jax.shard_map(
        per_device,
        mesh=mesh,
        in_specs=placed,
        out_specs=(P("freq", None, None, "space"), P("freq", None, None, None)),
        check_vma=False,
    )
```

```python
import functools
import math

import jax
import jax.numpy as jnp
from jax import lax
from jax.experimental import pallas as pl
from jax.experimental.pallas import tpu as pltpu
from jax.sharding import PartitionSpec as P

NFFT = 512
NBLK = 7
HALF = 4
SHIFTS = 9
ORDER = SHIFTS * NBLK
PAD = 64
LANES = 128
SPREAD = 2
SPAN = 136
PARTS = 2
OWN = PARTS * NBLK


def transform_table(freqs, alpha):
    sample_index = jnp.arange(NFFT, dtype=jnp.int32)
    shift_index = jnp.arange(SHIFTS, dtype=jnp.int32) - HALF
    freq_bins = jnp.mod(freqs[None, :] + shift_index[:, None] * alpha[0], NFFT)
    phase_steps = jnp.mod(freq_bins[:, :, None] * sample_index[None, None, :], NFFT)
    phase = phase_steps.astype(jnp.float32) * (2.0 * math.pi / NFFT)
    sample_float = sample_index.astype(jnp.float32)
    window_shape = 0.5 - 0.5 * jnp.cos(sample_float * (2.0 * math.pi / NFFT))
    window_scale = window_shape / jnp.sqrt(jnp.sum(window_shape * window_shape))
    real_part = window_scale * jnp.cos(phase)
    imag_part = -(window_scale * jnp.sin(phase))
    return jnp.stack([real_part, imag_part], axis=0).astype(jnp.bfloat16)


def middle_kernel(n_out, scalars_ref, mine_ref, other_ref, table_ref, out_ref, rows32, spec32, own32):
    quarters, spread_rows, _ = rows32.shape
    own_rows = OWN * quarters
    run = spread_rows // SPREAD // (2 * n_out)
    core = scalars_ref[NBLK]
    for quarter in range(quarters):
        lanes = slice(quarter * LANES, (quarter + 1) * LANES)
        for source in range(n_out):
            taken = slice(source * run, (source + 1) * run)
            for ref, side in ((mine_ref, core), (other_ref, 1 - core)):
                first = SPREAD * run * (2 * source + side)
                rows32[quarter, pl.ds(first, run, stride=SPREAD), :] = ref[taken, lanes].astype(jnp.float32)
        for part in range(PARTS):
            zero = jnp.zeros((n_out, LANES), jnp.float32)
            spec32[quarter, pl.ds(part * PAD + ORDER, n_out, stride=SPAN), :] = zero

    for block in range(NBLK):
        first = scalars_ref[block] * SPREAD
        block_rows = jnp.concatenate(
            [rows32[quarter, pl.ds(first, NFFT, stride=SPREAD), :] for quarter in range(quarters)], axis=1
        ).astype(jnp.bfloat16)
        spec = jnp.dot(table_ref[...], block_rows, preferred_element_type=jnp.float32)
        for part in range(PARTS):
            for shift in range(SHIFTS):
                base = (part * SHIFTS + shift) * n_out
                row = part * PAD + shift * NBLK + block
                for quarter in range(quarters):
                    values = spec[base : base + n_out, quarter * LANES : (quarter + 1) * LANES]
                    spec32[quarter, pl.ds(row, n_out, stride=SPAN), :] = values
                    if shift == HALF:
                        own_row = (part * NBLK + block) * quarters + quarter
                        own32[pl.ds(own_row, n_out, stride=own_rows), :] = values

    row_index = lax.broadcasted_iota(jnp.int32, (PAD, LANES), 0)
    lane_index = lax.broadcasted_iota(jnp.int32, (PAD, LANES), 1)
    low = lane_index < PAD
    column = jnp.where(low, lane_index, lane_index - PAD)
    keep = (row_index <= column) == low
    sign = jnp.where(low, 1.0, -1.0)
    low_half = low[: PAD // 2]

    def one_frequency(j, carry):
        first = pl.multiple_of(j * SPAN, 8)
        stacked = jnp.concatenate(
            [spec32[quarter, pl.ds(first, 2 * PAD), :] for quarter in range(quarters)], axis=1
        ).astype(jnp.bfloat16)
        products = lax.dot_general(
            stacked, stacked, (((1,), (1,)), ((), ())), preferred_element_type=jnp.float32
        )
        both = products[:PAD] + sign * pltpu.roll(products[PAD:], PAD, 1)
        merged = jnp.where(keep, both, pltpu.roll(both, PAD, 1))
        packed = jnp.where(low_half, merged[: PAD // 2], merged[PAD // 2 :])
        own = own32[pl.ds(pl.multiple_of(j * own_rows, 8), own_rows), :]
        out_ref[j] = jnp.concatenate([own, packed], axis=0).astype(jnp.bfloat16)
        return carry

    lax.fori_loop(0, n_out, one_frequency, 0, unroll=16)


def transform_and_gram(scalars, mine, other, table, n_out):
    run_rows, cells = mine.shape
    quarters = cells // LANES
    own_rows = OWN * quarters
    vmem = pl.BlockSpec(memory_space=pltpu.VMEM)
    flops = 2 * NBLK * table.shape[0] * NFFT * cells + 2 * n_out * (2 * PAD) ** 2 * cells
    return pl.pallas_call(
        functools.partial(middle_kernel, n_out),
        out_shape=jax.ShapeDtypeStruct((n_out, own_rows + PAD // 2, LANES), jnp.bfloat16),
        in_specs=[pl.BlockSpec(memory_space=pltpu.SMEM), vmem, vmem, vmem],
        out_specs=vmem,
        scratch_shapes=[
            pltpu.VMEM((quarters, 2 * run_rows * SPREAD, LANES), jnp.float32),
            pltpu.VMEM((quarters, n_out * SPAN, LANES), jnp.float32),
            pltpu.VMEM((n_out * own_rows, LANES), jnp.float32),
        ],
        cost_estimate=pl.CostEstimate(flops=flops, bytes_accessed=4 << 20, transcendentals=0),
        compiler_params=pltpu.CompilerParams(vmem_limit_bytes=32 << 20),
        name="transform_and_gram",
    )(scalars, mine, other, table)


def unpack_gram(packed):
    square = jnp.concatenate([packed[:, :PAD], packed[:, PAD:]], axis=0)[:ORDER, :ORDER]
    upper = jnp.arange(ORDER)[:, None] <= jnp.arange(ORDER)[None, :]
    diagonal = jnp.arange(ORDER)[:, None] == jnp.arange(ORDER)[None, :]
    real_gram = jnp.where(upper, square, square.T)
    imag_gram = jnp.where(upper, jnp.where(diagonal, 0.0, -square.T), square)
    return jnp.stack([real_gram, imag_gram], axis=0)


def per_device(series, starts, freqs, alpha):
    slab_cells = series.shape[1]
    n_space = lax.axis_size("space")
    n_freq = freqs.shape[0]
    n_out = n_freq // 2
    total_cells = slab_cells * n_space
    cells = slab_cells // n_out
    quarters = cells // LANES
    core = lax.rem(lax.axis_index("freq"), 2)
    same_core = [[2 * chip + side for chip in range(n_out)] for side in range(2)]

    mine = lax.all_to_all(
        series, "freq", split_axis=1, concat_axis=0, tiled=True, axis_index_groups=same_core
    )
    own_freqs = jnp.where(core == 0, freqs[0::2], freqs[1::2])
    table = transform_table(own_freqs, alpha).reshape(PARTS * SHIFTS * n_out, NFFT)
    scalars = jnp.concatenate([starts, core[None].astype(starts.dtype)])
    mine, table, scalars = lax.optimization_barrier((mine, table, scalars))
    other = lax.ppermute(mine, "freq", [(index, index ^ 1) for index in range(n_freq)])
    message = transform_and_gram(scalars, mine, other, table, n_out)
    received = lax.all_to_all(
        message, "freq", split_axis=0, concat_axis=0, tiled=True, axis_index_groups=same_core
    )
    own = received[:, : OWN * quarters].reshape(n_out, PARTS, NBLK, cells)
    spectra = jnp.transpose(own, (1, 2, 0, 3)).reshape(1, PARTS, NBLK, slab_cells)
    slab_gram = jnp.sum(received[:, OWN * quarters :].astype(jnp.float32), axis=0)
    spread = jnp.broadcast_to(slab_gram[None], (n_space, PAD // 2, LANES))
    slabs = lax.all_to_all(spread, "space", split_axis=0, concat_axis=0, tiled=True)
    gram = unpack_gram(jnp.sum(slabs, axis=0) / total_cells)[None]
    return (spectra, gram)


def solution(mesh):
    placed = (P("freq", "space"), P(), P(), P())
    return jax.shard_map(
        per_device,
        mesh=mesh,
        in_specs=placed,
        out_specs=(P("freq", None, None, "space"), P("freq", None, None, None)),
        check_vma=False,
    )
```

```python
import functools
import math

import jax
import jax.numpy as jnp
from jax import lax
from jax.experimental import pallas as pl
from jax.experimental.pallas import tpu as pltpu
from jax.sharding import PartitionSpec as P

NFFT = 512
NBLK = 7
HALF = 4
SHIFTS = 9
ORDER = SHIFTS * NBLK
PAD = 64
LANES = 128
SPREAD = 2
SPAN = 136
PARTS = 2
OWN = PARTS * NBLK


def transform_table(freqs, alpha):
    sample_index = jnp.arange(NFFT, dtype=jnp.int32)
    shift_index = jnp.arange(SHIFTS, dtype=jnp.int32) - HALF
    freq_bins = jnp.mod(freqs[None, :] + shift_index[:, None] * alpha[0], NFFT)
    phase_steps = jnp.mod(freq_bins[:, :, None] * sample_index[None, None, :], NFFT)
    phase = phase_steps.astype(jnp.float32) * (2.0 * math.pi / NFFT)
    sample_float = sample_index.astype(jnp.float32)
    window_shape = 0.5 - 0.5 * jnp.cos(sample_float * (2.0 * math.pi / NFFT))
    window_scale = window_shape / jnp.sqrt(jnp.sum(window_shape * window_shape))
    real_part = window_scale * jnp.cos(phase)
    imag_part = -(window_scale * jnp.sin(phase))
    return jnp.stack([real_part, imag_part], axis=0).astype(jnp.bfloat16)


def middle_kernel(n_out, scalars_ref, mine_ref, other_ref, table_ref, out_ref, rows32, spec32, own32):
    quarters, spread_rows, _ = rows32.shape
    own_rows = OWN * quarters
    run = spread_rows // SPREAD // (2 * n_out)
    core = scalars_ref[NBLK]
    for quarter in range(quarters):
        lanes = slice(quarter * LANES, (quarter + 1) * LANES)
        for source in range(n_out):
            taken = slice(source * run, (source + 1) * run)
            for ref, side in ((mine_ref, core), (other_ref, 1 - core)):
                first = SPREAD * run * (2 * source + side)
                rows32[quarter, pl.ds(first, run, stride=SPREAD), :] = ref[taken, lanes].astype(jnp.float32)
        for part in range(PARTS):
            zero = jnp.zeros((n_out, LANES), jnp.float32)
            spec32[quarter, pl.ds(part * PAD + ORDER, n_out, stride=SPAN), :] = zero

    for block in range(NBLK):
        first = scalars_ref[block] * SPREAD
        block_rows = jnp.concatenate(
            [rows32[quarter, pl.ds(first, NFFT, stride=SPREAD), :] for quarter in range(quarters)], axis=1
        ).astype(jnp.bfloat16)
        spec = jnp.dot(table_ref[...], block_rows, preferred_element_type=jnp.float32)
        for part in range(PARTS):
            for shift in range(SHIFTS):
                base = (part * SHIFTS + shift) * n_out
                row = part * PAD + shift * NBLK + block
                for quarter in range(quarters):
                    values = spec[base : base + n_out, quarter * LANES : (quarter + 1) * LANES]
                    spec32[quarter, pl.ds(row, n_out, stride=SPAN), :] = values
                    if shift == HALF:
                        own_row = (part * NBLK + block) * quarters + quarter
                        own32[pl.ds(own_row, n_out, stride=own_rows), :] = values

    row_index = lax.broadcasted_iota(jnp.int32, (PAD, LANES), 0)
    lane_index = lax.broadcasted_iota(jnp.int32, (PAD, LANES), 1)
    low = lane_index < PAD
    column = jnp.where(low, lane_index, lane_index - PAD)
    keep = (row_index <= column) == low
    sign = jnp.where(low, 1.0, -1.0)
    low_half = low[: PAD // 2]

    def one_frequency(j, carry):
        first = pl.multiple_of(j * SPAN, 8)
        stacked = jnp.concatenate(
            [spec32[quarter, pl.ds(first, 2 * PAD), :] for quarter in range(quarters)], axis=1
        ).astype(jnp.bfloat16)
        products = lax.dot_general(
            stacked, stacked, (((1,), (1,)), ((), ())), preferred_element_type=jnp.float32
        )
        both = products[:PAD] + sign * pltpu.roll(products[PAD:], PAD, 1)
        merged = jnp.where(keep, both, pltpu.roll(both, PAD, 1))
        packed = jnp.where(low_half, merged[: PAD // 2], merged[PAD // 2 :])
        own = own32[pl.ds(pl.multiple_of(j * own_rows, 8), own_rows), :]
        out_ref[j] = jnp.concatenate([own, packed], axis=0).astype(jnp.bfloat16)
        return carry

    lax.fori_loop(0, n_out, one_frequency, 0, unroll=16)


def transform_and_gram(scalars, mine, other, table, n_out):
    run_rows, cells = mine.shape
    quarters = cells // LANES
    own_rows = OWN * quarters
    vmem = pl.BlockSpec(memory_space=pltpu.VMEM)
    flops = 2 * NBLK * table.shape[0] * NFFT * cells + 2 * n_out * (2 * PAD) ** 2 * cells
    return pl.pallas_call(
        functools.partial(middle_kernel, n_out),
        out_shape=jax.ShapeDtypeStruct((n_out, own_rows + PAD // 2, LANES), jnp.bfloat16),
        in_specs=[pl.BlockSpec(memory_space=pltpu.SMEM), vmem, vmem, vmem],
        out_specs=vmem,
        scratch_shapes=[
            pltpu.VMEM((quarters, 2 * run_rows * SPREAD, LANES), jnp.float32),
            pltpu.VMEM((quarters, n_out * SPAN, LANES), jnp.float32),
            pltpu.VMEM((n_out * own_rows, LANES), jnp.float32),
        ],
        cost_estimate=pl.CostEstimate(flops=flops, bytes_accessed=4 << 20, transcendentals=0),
        compiler_params=pltpu.CompilerParams(vmem_limit_bytes=32 << 20),
        name="transform_and_gram",
    )(scalars, mine, other, table)


def unpack_gram(packed):
    square = jnp.concatenate([packed[:, :PAD], packed[:, PAD:]], axis=0)[:ORDER, :ORDER]
    upper = jnp.arange(ORDER)[:, None] <= jnp.arange(ORDER)[None, :]
    diagonal = jnp.arange(ORDER)[:, None] == jnp.arange(ORDER)[None, :]
    real_gram = jnp.where(upper, square, square.T)
    imag_gram = jnp.where(upper, jnp.where(diagonal, 0.0, -square.T), square)
    return jnp.stack([real_gram, imag_gram], axis=0)


def per_device(series, starts, freqs, alpha):
    slab_cells = series.shape[1]
    n_space = lax.axis_size("space")
    n_freq = freqs.shape[0]
    n_out = n_freq // 2
    total_cells = slab_cells * n_space
    cells = slab_cells // n_out
    quarters = cells // LANES
    core = lax.rem(lax.axis_index("freq"), 2)
    same_core = [[2 * chip + side for chip in range(n_out)] for side in range(2)]

    mine = lax.all_to_all(
        series, "freq", split_axis=1, concat_axis=0, tiled=True, axis_index_groups=same_core
    )
    own_freqs = jnp.where(core == 0, freqs[0::2], freqs[1::2])
    table = transform_table(own_freqs, alpha).reshape(PARTS * SHIFTS * n_out, NFFT)
    scalars = jnp.concatenate([starts, core[None].astype(starts.dtype)])
    mine, table, scalars = lax.optimization_barrier((mine, table, scalars))
    other = lax.ppermute(mine, "freq", [(index, index ^ 1) for index in range(n_freq)])
    message = transform_and_gram(scalars, mine, other, table, n_out)
    received = lax.all_to_all(
        message, "freq", split_axis=0, concat_axis=0, tiled=True, axis_index_groups=same_core
    )
    own = received[:, : OWN * quarters].reshape(n_out, PARTS, NBLK, cells)
    spectra = jnp.transpose(own, (1, 2, 0, 3)).reshape(1, PARTS, NBLK, slab_cells)
    slab_gram = jnp.sum(received[:, OWN * quarters :].astype(jnp.float32), axis=0).astype(jnp.bfloat16)
    spread = jnp.broadcast_to(slab_gram[None], (n_space, PAD // 2, LANES))
    slabs = lax.all_to_all(spread, "space", split_axis=0, concat_axis=0, tiled=True)
    gram = unpack_gram(jnp.sum(slabs.astype(jnp.float32), axis=0) / total_cells)[None]
    return (spectra, gram)


def solution(mesh):
    placed = (P("freq", "space"), P(), P(), P())
    return jax.shard_map(
        per_device,
        mesh=mesh,
        in_specs=placed,
        out_specs=(P("freq", None, None, "space"), P("freq", None, None, None)),
        check_vma=False,
    )
```

```python
import functools
import math

import jax
import jax.numpy as jnp
from jax import lax
from jax.experimental import pallas as pl
from jax.experimental.pallas import tpu as pltpu
from jax.sharding import PartitionSpec as P

NFFT = 512
NBLK = 7
HALF = 4
SHIFTS = 9
ORDER = SHIFTS * NBLK
PAD = 64
LANES = 128
SPREAD = 2
SPAN = 136
PARTS = 2
OWN = PARTS * NBLK


def transform_table(freqs, alpha):
    sample_index = jnp.arange(NFFT, dtype=jnp.int32)
    shift_index = jnp.arange(SHIFTS, dtype=jnp.int32) - HALF
    freq_bins = jnp.mod(freqs[None, :] + shift_index[:, None] * alpha[0], NFFT)
    phase_steps = jnp.mod(freq_bins[:, :, None] * sample_index[None, None, :], NFFT)
    phase = phase_steps.astype(jnp.float32) * (2.0 * math.pi / NFFT)
    sample_float = sample_index.astype(jnp.float32)
    window_shape = 0.5 - 0.5 * jnp.cos(sample_float * (2.0 * math.pi / NFFT))
    window_scale = window_shape / jnp.sqrt(jnp.sum(window_shape * window_shape))
    real_part = window_scale * jnp.cos(phase)
    imag_part = -(window_scale * jnp.sin(phase))
    return jnp.stack([real_part, imag_part], axis=0).astype(jnp.bfloat16)


def middle_kernel(n_out, piece_rows, scalars_ref, mine_ref, other_ref, table_ref, own_ref, gram_ref,
                  rows32, spec32, own32, gram32):
    quarters, spread_rows, _ = rows32.shape
    own_rows = OWN * quarters
    run = spread_rows // SPREAD // (2 * n_out)
    core = scalars_ref[NBLK]
    for quarter in range(quarters):
        lanes = slice(quarter * LANES, (quarter + 1) * LANES)
        for source in range(n_out):
            taken = slice(source * run, (source + 1) * run)
            for ref, side in ((mine_ref, core), (other_ref, 1 - core)):
                first = SPREAD * run * (2 * source + side)
                rows32[quarter, pl.ds(first, run, stride=SPREAD), :] = ref[taken, lanes].astype(jnp.float32)
        for part in range(PARTS):
            zero = jnp.zeros((n_out, LANES), jnp.float32)
            spec32[quarter, pl.ds(part * PAD + ORDER, n_out, stride=SPAN), :] = zero

    for block in range(NBLK):
        first = scalars_ref[block] * SPREAD
        block_rows = jnp.concatenate(
            [rows32[quarter, pl.ds(first, NFFT, stride=SPREAD), :] for quarter in range(quarters)], axis=1
        ).astype(jnp.bfloat16)
        spec = jnp.dot(table_ref[...], block_rows, preferred_element_type=jnp.float32)
        for part in range(PARTS):
            for shift in range(SHIFTS):
                base = (part * SHIFTS + shift) * n_out
                row = part * PAD + shift * NBLK + block
                for quarter in range(quarters):
                    values = spec[base : base + n_out, quarter * LANES : (quarter + 1) * LANES]
                    spec32[quarter, pl.ds(row, n_out, stride=SPAN), :] = values
                    if shift == HALF:
                        own_row = (part * NBLK + block) * quarters + quarter
                        own32[pl.ds(own_row, n_out, stride=own_rows), :] = values

    row_index = lax.broadcasted_iota(jnp.int32, (PAD, LANES), 0)
    lane_index = lax.broadcasted_iota(jnp.int32, (PAD, LANES), 1)
    low = lane_index < PAD
    column = jnp.where(low, lane_index, lane_index - PAD)
    keep = (row_index <= column) == low
    sign = jnp.where(low, 1.0, -1.0)
    low_half = low[: PAD // 2]

    def one_frequency(j, carry):
        first = pl.multiple_of(j * SPAN, 8)
        stacked = jnp.concatenate(
            [spec32[quarter, pl.ds(first, 2 * PAD), :] for quarter in range(quarters)], axis=1
        ).astype(jnp.bfloat16)
        products = lax.dot_general(
            stacked, stacked, (((1,), (1,)), ((), ())), preferred_element_type=jnp.float32
        )
        both = products[:PAD] + sign * pltpu.roll(products[PAD:], PAD, 1)
        merged = jnp.where(keep, both, pltpu.roll(both, PAD, 1))
        packed = jnp.where(low_half, merged[: PAD // 2], merged[PAD // 2 :])
        own = own32[pl.ds(pl.multiple_of(j * own_rows, 8), own_rows), :]
        own_ref[j] = own.astype(jnp.bfloat16)
        for p in range(PAD // 2 // piece_rows):
            target = (p * n_out + j) * piece_rows
            gram32[pl.ds(target, piece_rows), :] = packed[p * piece_rows : (p + 1) * piece_rows]
        return carry

    lax.fori_loop(0, n_out, one_frequency, 0, unroll=16)
    gram_ref[...] = gram32[...].astype(jnp.bfloat16)


def transform_and_gram(scalars, mine, other, table, n_out, piece_rows):
    run_rows, cells = mine.shape
    quarters = cells // LANES
    own_rows = OWN * quarters
    vmem = pl.BlockSpec(memory_space=pltpu.VMEM)
    flops = 2 * NBLK * table.shape[0] * NFFT * cells + 2 * n_out * (2 * PAD) ** 2 * cells
    return pl.pallas_call(
        functools.partial(middle_kernel, n_out, piece_rows),
        out_shape=(
            jax.ShapeDtypeStruct((n_out, own_rows, LANES), jnp.bfloat16),
            jax.ShapeDtypeStruct((n_out * PAD // 2, LANES), jnp.bfloat16),
        ),
        in_specs=[pl.BlockSpec(memory_space=pltpu.SMEM), vmem, vmem, vmem],
        out_specs=(vmem, vmem),
        scratch_shapes=[
            pltpu.VMEM((quarters, 2 * run_rows * SPREAD, LANES), jnp.float32),
            pltpu.VMEM((quarters, n_out * SPAN, LANES), jnp.float32),
            pltpu.VMEM((n_out * own_rows, LANES), jnp.float32),
            pltpu.VMEM((n_out * PAD // 2, LANES), jnp.float32),
        ],
        cost_estimate=pl.CostEstimate(flops=flops, bytes_accessed=4 << 20, transcendentals=0),
        compiler_params=pltpu.CompilerParams(vmem_limit_bytes=32 << 20),
        name="transform_and_gram",
    )(scalars, mine, other, table)


def unpack_gram(packed):
    square = jnp.concatenate([packed[:, :PAD], packed[:, PAD:]], axis=0)[:ORDER, :ORDER]
    upper = jnp.arange(ORDER)[:, None] <= jnp.arange(ORDER)[None, :]
    diagonal = jnp.arange(ORDER)[:, None] == jnp.arange(ORDER)[None, :]
    real_gram = jnp.where(upper, square, square.T)
    imag_gram = jnp.where(upper, jnp.where(diagonal, 0.0, -square.T), square)
    return jnp.stack([real_gram, imag_gram], axis=0)


def per_device(series, starts, freqs, alpha):
    slab_cells = series.shape[1]
    n_space = lax.axis_size("space")
    n_freq = freqs.shape[0]
    n_out = n_freq // 2
    total_cells = slab_cells * n_space
    cells = slab_cells // n_out
    quarters = cells // LANES
    piece_rows = PAD // 2 // n_space
    core = lax.rem(lax.axis_index("freq"), 2)
    same_core = [[2 * chip + side for chip in range(n_out)] for side in range(2)]

    mine = lax.all_to_all(
        series, "freq", split_axis=1, concat_axis=0, tiled=True, axis_index_groups=same_core
    )
    own_freqs = jnp.where(core == 0, freqs[0::2], freqs[1::2])
    table = transform_table(own_freqs, alpha).reshape(PARTS * SHIFTS * n_out, NFFT)
    scalars = jnp.concatenate([starts, core[None].astype(starts.dtype)])
    mine, table, scalars = lax.optimization_barrier((mine, table, scalars))
    other = lax.ppermute(mine, "freq", [(index, index ^ 1) for index in range(n_freq)])
    own, partial = transform_and_gram(scalars, mine, other, table, n_out, piece_rows)
    partial = partial.reshape(n_space, n_out * piece_rows, LANES)
    gathered = lax.all_to_all(partial, "space", split_axis=0, concat_axis=0, tiled=True)
    piece_sum = jnp.sum(gathered.astype(jnp.float32), axis=0).astype(jnp.bfloat16)
    message = jnp.concatenate([own, piece_sum.reshape(n_out, piece_rows, LANES)], axis=1)
    received = lax.all_to_all(
        message, "freq", split_axis=0, concat_axis=0, tiled=True, axis_index_groups=same_core
    )
    own = received[:, : OWN * quarters].reshape(n_out, PARTS, NBLK, cells)
    spectra = jnp.transpose(own, (1, 2, 0, 3)).reshape(1, PARTS, NBLK, slab_cells)
    gram_piece = jnp.sum(received[:, OWN * quarters :].astype(jnp.float32), axis=0)
    spread = jnp.broadcast_to(gram_piece[None], (n_space, piece_rows, LANES))
    pieces = lax.all_to_all(spread, "space", split_axis=0, concat_axis=0, tiled=True)
    gram = unpack_gram(pieces.reshape(PAD // 2, LANES) / total_cells)[None]
    return (spectra, gram)


def solution(mesh):
    placed = (P("freq", "space"), P(), P(), P())
    return jax.shard_map(
        per_device,
        mesh=mesh,
        in_specs=placed,
        out_specs=(P("freq", None, None, "space"), P("freq", None, None, None)),
        check_vma=False,
    )
```

```python
import functools
import math

import jax
import jax.numpy as jnp
from jax import lax
from jax.experimental import pallas as pl
from jax.experimental.pallas import tpu as pltpu
from jax.sharding import PartitionSpec as P

NFFT = 512
NBLK = 7
HALF = 4
SHIFTS = 9
ORDER = SHIFTS * NBLK
PAD = 64
LANES = 128
SPREAD = 2
SPAN = 136
PARTS = 2
OWN = PARTS * NBLK


def transform_table(freqs, alpha):
    sample_index = jnp.arange(NFFT, dtype=jnp.int32)
    shift_index = jnp.arange(SHIFTS, dtype=jnp.int32) - HALF
    freq_bins = jnp.mod(freqs[None, :] + shift_index[:, None] * alpha[0], NFFT)
    phase_steps = jnp.mod(freq_bins[:, :, None] * sample_index[None, None, :], NFFT)
    phase = phase_steps.astype(jnp.float32) * (2.0 * math.pi / NFFT)
    sample_float = sample_index.astype(jnp.float32)
    window_shape = 0.5 - 0.5 * jnp.cos(sample_float * (2.0 * math.pi / NFFT))
    window_scale = window_shape / jnp.sqrt(jnp.sum(window_shape * window_shape))
    real_part = window_scale * jnp.cos(phase)
    imag_part = -(window_scale * jnp.sin(phase))
    return jnp.stack([real_part, imag_part], axis=0).astype(jnp.bfloat16)


def middle_kernel(n_out, scalars_ref, mine_ref, other_ref, table_ref, out_ref, rows32, spec32, own32):
    quarters, spread_rows, _ = rows32.shape
    own_rows = OWN * quarters
    run = spread_rows // SPREAD // (2 * n_out)
    core = scalars_ref[NBLK]
    even = core == 0

    def aligned_rows(first_row):
        pieces = []
        for source in range(first_row // (2 * run), (first_row + NFFT) // (2 * run)):
            taken = slice(source * run, (source + 1) * run)
            mine, other = mine_ref[taken, :], other_ref[taken, :]
            pieces += [jnp.where(even, mine, other), jnp.where(even, other, mine)]
        return jnp.concatenate(pieces, axis=0)

    for quarter in range(quarters):
        lanes = slice(quarter * LANES, (quarter + 1) * LANES)
        for source in range(n_out):
            taken = slice(source * run, (source + 1) * run)
            for ref, side in ((mine_ref, core), (other_ref, 1 - core)):
                first = SPREAD * run * (2 * source + side)
                rows32[quarter, pl.ds(first, run, stride=SPREAD), :] = ref[taken, lanes].astype(jnp.float32)
        for part in range(PARTS):
            zero = jnp.zeros((n_out, LANES), jnp.float32)
            spec32[quarter, pl.ds(part * PAD + ORDER, n_out, stride=SPAN), :] = zero

    for block in range(NBLK):
        first = scalars_ref[block] * SPREAD
        if block == 0:
            block_rows = aligned_rows(0)
        elif block == NBLK - 1:
            block_rows = aligned_rows(2 * run * n_out - NFFT)
        else:
            block_rows = jnp.concatenate(
                [rows32[quarter, pl.ds(first, NFFT, stride=SPREAD), :] for quarter in range(quarters)], axis=1
            ).astype(jnp.bfloat16)
        spec = jnp.dot(table_ref[...], block_rows, preferred_element_type=jnp.float32)
        for part in range(PARTS):
            for shift in range(SHIFTS):
                base = (part * SHIFTS + shift) * n_out
                row = part * PAD + shift * NBLK + block
                for quarter in range(quarters):
                    values = spec[base : base + n_out, quarter * LANES : (quarter + 1) * LANES]
                    spec32[quarter, pl.ds(row, n_out, stride=SPAN), :] = values
                    if shift == HALF:
                        own_row = (part * NBLK + block) * quarters + quarter
                        own32[pl.ds(own_row, n_out, stride=own_rows), :] = values

    row_index = lax.broadcasted_iota(jnp.int32, (PAD, LANES), 0)
    lane_index = lax.broadcasted_iota(jnp.int32, (PAD, LANES), 1)
    low = lane_index < PAD
    column = jnp.where(low, lane_index, lane_index - PAD)
    keep = (row_index <= column) == low
    sign = jnp.where(low, 1.0, -1.0)
    low_half = low[: PAD // 2]

    def one_frequency(j, carry):
        first = pl.multiple_of(j * SPAN, 8)
        stacked = jnp.concatenate(
            [spec32[quarter, pl.ds(first, 2 * PAD), :] for quarter in range(quarters)], axis=1
        ).astype(jnp.bfloat16)
        products = lax.dot_general(
            stacked, stacked, (((1,), (1,)), ((), ())), preferred_element_type=jnp.float32
        )
        both = products[:PAD] + sign * pltpu.roll(products[PAD:], PAD, 1)
        merged = jnp.where(keep, both, pltpu.roll(both, PAD, 1))
        packed = jnp.where(low_half, merged[: PAD // 2], merged[PAD // 2 :])
        own = own32[pl.ds(pl.multiple_of(j * own_rows, 8), own_rows), :]
        out_ref[j] = jnp.concatenate([own, packed], axis=0).astype(jnp.bfloat16)
        return carry

    lax.fori_loop(0, n_out, one_frequency, 0, unroll=16)


def transform_and_gram(scalars, mine, other, table, n_out):
    run_rows, cells = mine.shape
    quarters = cells // LANES
    own_rows = OWN * quarters
    vmem = pl.BlockSpec(memory_space=pltpu.VMEM)
    flops = 2 * NBLK * table.shape[0] * NFFT * cells + 2 * n_out * (2 * PAD) ** 2 * cells
    return pl.pallas_call(
        functools.partial(middle_kernel, n_out),
        out_shape=jax.ShapeDtypeStruct((n_out, own_rows + PAD // 2, LANES), jnp.bfloat16),
        in_specs=[pl.BlockSpec(memory_space=pltpu.SMEM), vmem, vmem, vmem],
        out_specs=vmem,
        scratch_shapes=[
            pltpu.VMEM((quarters, 2 * run_rows * SPREAD, LANES), jnp.float32),
            pltpu.VMEM((quarters, n_out * SPAN, LANES), jnp.float32),
            pltpu.VMEM((n_out * own_rows, LANES), jnp.float32),
        ],
        cost_estimate=pl.CostEstimate(flops=flops, bytes_accessed=4 << 20, transcendentals=0),
        compiler_params=pltpu.CompilerParams(vmem_limit_bytes=32 << 20),
        name="transform_and_gram",
    )(scalars, mine, other, table)


def split_kernel(series_ref, chunks_ref):
    count, _, cells = chunks_ref.shape
    for chunk in range(count):
        chunks_ref[chunk] = series_ref[:, chunk * cells : (chunk + 1) * cells]


def split_cells(series, n_chunks):
    rows, slab_cells = series.shape
    cells, step = slab_cells // n_chunks, n_chunks // 2
    return pl.pallas_call(
        split_kernel,
        grid=(2,),
        out_shape=jax.ShapeDtypeStruct((n_chunks, rows, cells), series.dtype),
        in_specs=[pl.BlockSpec((rows, step * cells), lambda i: (0, i))],
        out_specs=pl.BlockSpec((step, rows, cells), lambda i: (i, 0, 0)),
        name="split_cells",
    )(series)


def unpack_gram(packed):
    square = jnp.concatenate([packed[:, :PAD], packed[:, PAD:]], axis=0)[:ORDER, :ORDER]
    upper = jnp.arange(ORDER)[:, None] <= jnp.arange(ORDER)[None, :]
    diagonal = jnp.arange(ORDER)[:, None] == jnp.arange(ORDER)[None, :]
    real_gram = jnp.where(upper, square, square.T)
    imag_gram = jnp.where(upper, jnp.where(diagonal, 0.0, -square.T), square)
    return jnp.stack([real_gram, imag_gram], axis=0)


def per_device(series, starts, freqs, alpha):
    slab_cells = series.shape[1]
    n_space = lax.axis_size("space")
    n_freq = freqs.shape[0]
    n_out = n_freq // 2
    total_cells = slab_cells * n_space
    cells = slab_cells // n_out
    quarters = cells // LANES
    core = lax.rem(lax.axis_index("freq"), 2)
    same_core = [[2 * chip + side for chip in range(n_out)] for side in range(2)]

    mine = lax.all_to_all(
        split_cells(series, n_out), "freq", split_axis=0, concat_axis=0, tiled=True, axis_index_groups=same_core
    ).reshape(-1, cells)
    own_freqs = jnp.where(core == 0, freqs[0::2], freqs[1::2])
    table = transform_table(own_freqs, alpha).reshape(PARTS * SHIFTS * n_out, NFFT)
    scalars = jnp.concatenate([starts, core[None].astype(starts.dtype)])
    mine, table, scalars = lax.optimization_barrier((mine, table, scalars))
    other = lax.ppermute(mine, "freq", [(index, index ^ 1) for index in range(n_freq)])
    message = transform_and_gram(scalars, mine, other, table, n_out)
    received = lax.all_to_all(
        message, "freq", split_axis=0, concat_axis=0, tiled=True, axis_index_groups=same_core
    )
    own = received[:, : OWN * quarters].reshape(n_out, PARTS, NBLK, cells)
    spectra = jnp.transpose(own, (1, 2, 0, 3)).reshape(1, PARTS, NBLK, slab_cells)
    slab_gram = jnp.sum(received[:, OWN * quarters :].astype(jnp.float32), axis=0)
    spread = jnp.broadcast_to(slab_gram[None], (n_space, PAD // 2, LANES))
    slabs = lax.all_to_all(spread, "space", split_axis=0, concat_axis=0, tiled=True)
    gram = unpack_gram(jnp.sum(slabs, axis=0) / total_cells)[None]
    return (spectra, gram)


def solution(mesh):
    placed = (P("freq", "space"), P(), P(), P())
    return jax.shard_map(
        per_device,
        mesh=mesh,
        in_specs=placed,
        out_specs=(P("freq", None, None, "space"), P("freq", None, None, None)),
        check_vma=False,
    )
```

```python
import functools
import math

import jax
import jax.numpy as jnp
from jax import lax
from jax.experimental import pallas as pl
from jax.experimental.pallas import tpu as pltpu
from jax.sharding import PartitionSpec as P

NFFT = 512
NBLK = 7
HALF = 4
SHIFTS = 9
ORDER = SHIFTS * NBLK
PAD = 64
LANES = 128
SPREAD = 2
SPAN = 136
PARTS = 2
OWN = PARTS * NBLK


def transform_table(freqs, alpha):
    sample_index = jnp.arange(NFFT, dtype=jnp.int32)
    shift_index = jnp.arange(SHIFTS, dtype=jnp.int32) - HALF
    freq_bins = jnp.mod(freqs[None, :] + shift_index[:, None] * alpha[0], NFFT)
    phase_steps = jnp.mod(freq_bins[:, :, None] * sample_index[None, None, :], NFFT)
    phase = phase_steps.astype(jnp.float32) * (2.0 * math.pi / NFFT)
    sample_float = sample_index.astype(jnp.float32)
    window_shape = 0.5 - 0.5 * jnp.cos(sample_float * (2.0 * math.pi / NFFT))
    window_scale = window_shape / jnp.sqrt(jnp.sum(window_shape * window_shape))
    real_part = window_scale * jnp.cos(phase)
    imag_part = -(window_scale * jnp.sin(phase))
    return jnp.stack([real_part, imag_part], axis=0).astype(jnp.bfloat16)


def middle_kernel(n_out, scalars_ref, mine_ref, other_ref, table_ref, out_ref, rows32, spec32, own32):
    quarters, spread_rows, _ = rows32.shape
    own_rows = OWN * quarters
    run = spread_rows // SPREAD // (2 * n_out)
    core = scalars_ref[NBLK]
    even = core == 0

    def aligned_rows(first_row):
        pieces = []
        for source in range(first_row // (2 * run), (first_row + NFFT) // (2 * run)):
            taken = slice(source * run, (source + 1) * run)
            mine, other = mine_ref[taken, :], other_ref[taken, :]
            pieces += [jnp.where(even, mine, other), jnp.where(even, other, mine)]
        return jnp.concatenate(pieces, axis=0)

    for quarter in range(quarters):
        lanes = slice(quarter * LANES, (quarter + 1) * LANES)
        for source in range(n_out):
            taken = slice(source * run, (source + 1) * run)
            for ref, side in ((mine_ref, core), (other_ref, 1 - core)):
                first = SPREAD * run * (2 * source + side)
                rows32[quarter, pl.ds(first, run, stride=SPREAD), :] = ref[taken, lanes].astype(jnp.float32)
        for part in range(PARTS):
            zero = jnp.zeros((n_out, LANES), jnp.float32)
            spec32[quarter, pl.ds(part * PAD + ORDER, n_out, stride=SPAN), :] = zero

    for block in range(NBLK):
        first = scalars_ref[block] * SPREAD
        if block == 0:
            block_rows = aligned_rows(0)
        elif block == NBLK - 1:
            block_rows = aligned_rows(2 * run * n_out - NFFT)
        else:
            block_rows = jnp.concatenate(
                [rows32[quarter, pl.ds(first, NFFT, stride=SPREAD), :] for quarter in range(quarters)], axis=1
            ).astype(jnp.bfloat16)
        spec = jnp.dot(table_ref[...], block_rows, preferred_element_type=jnp.float32)
        for part in range(PARTS):
            for shift in range(SHIFTS):
                base = (part * SHIFTS + shift) * n_out
                row = part * PAD + shift * NBLK + block
                for quarter in range(quarters):
                    values = spec[base : base + n_out, quarter * LANES : (quarter + 1) * LANES]
                    spec32[quarter, pl.ds(row, n_out, stride=SPAN), :] = values
                    if shift == HALF:
                        own_row = (part * NBLK + block) * quarters + quarter
                        own32[pl.ds(own_row, n_out, stride=own_rows), :] = values

    row_index = lax.broadcasted_iota(jnp.int32, (PAD, LANES), 0)
    lane_index = lax.broadcasted_iota(jnp.int32, (PAD, LANES), 1)
    low = lane_index < PAD
    column = jnp.where(low, lane_index, lane_index - PAD)
    keep = (row_index <= column) == low
    sign = jnp.where(low, 1.0, -1.0)
    low_half = low[: PAD // 2]

    def one_frequency(j, carry):
        first = pl.multiple_of(j * SPAN, 8)
        stacked = jnp.concatenate(
            [spec32[quarter, pl.ds(first, 2 * PAD), :] for quarter in range(quarters)], axis=1
        ).astype(jnp.bfloat16)
        products = lax.dot_general(
            stacked, stacked, (((1,), (1,)), ((), ())), preferred_element_type=jnp.float32
        )
        both = products[:PAD] + sign * pltpu.roll(products[PAD:], PAD, 1)
        merged = jnp.where(keep, both, pltpu.roll(both, PAD, 1))
        packed = jnp.where(low_half, merged[: PAD // 2], merged[PAD // 2 :])
        own = own32[pl.ds(pl.multiple_of(j * own_rows, 8), own_rows), :]
        out_ref[j] = jnp.concatenate([own, packed], axis=0).astype(jnp.bfloat16)
        return carry

    lax.fori_loop(0, n_out, one_frequency, 0, unroll=32)


def transform_and_gram(scalars, mine, other, table, n_out):
    run_rows, cells = mine.shape
    quarters = cells // LANES
    own_rows = OWN * quarters
    vmem = pl.BlockSpec(memory_space=pltpu.VMEM)
    flops = 2 * NBLK * table.shape[0] * NFFT * cells + 2 * n_out * (2 * PAD) ** 2 * cells
    return pl.pallas_call(
        functools.partial(middle_kernel, n_out),
        out_shape=jax.ShapeDtypeStruct((n_out, own_rows + PAD // 2, LANES), jnp.bfloat16),
        in_specs=[pl.BlockSpec(memory_space=pltpu.SMEM), vmem, vmem, vmem],
        out_specs=vmem,
        scratch_shapes=[
            pltpu.VMEM((quarters, 2 * run_rows * SPREAD, LANES), jnp.float32),
            pltpu.VMEM((quarters, n_out * SPAN, LANES), jnp.float32),
            pltpu.VMEM((n_out * own_rows, LANES), jnp.float32),
        ],
        cost_estimate=pl.CostEstimate(flops=flops, bytes_accessed=4 << 20, transcendentals=0),
        compiler_params=pltpu.CompilerParams(vmem_limit_bytes=32 << 20),
        name="transform_and_gram",
    )(scalars, mine, other, table)


def split_kernel(series_ref, chunks_ref):
    count, _, cells = chunks_ref.shape
    for chunk in range(count):
        chunks_ref[chunk] = series_ref[:, chunk * cells : (chunk + 1) * cells]


def split_cells(series, n_chunks):
    rows, slab_cells = series.shape
    cells, step = slab_cells // n_chunks, n_chunks // 2
    return pl.pallas_call(
        split_kernel,
        grid=(2,),
        out_shape=jax.ShapeDtypeStruct((n_chunks, rows, cells), series.dtype),
        in_specs=[pl.BlockSpec((rows, step * cells), lambda i: (0, i))],
        out_specs=pl.BlockSpec((step, rows, cells), lambda i: (i, 0, 0)),
        name="split_cells",
    )(series)


def unpack_gram(packed):
    square = jnp.concatenate([packed[:, :PAD], packed[:, PAD:]], axis=0)[:ORDER, :ORDER]
    upper = jnp.arange(ORDER)[:, None] <= jnp.arange(ORDER)[None, :]
    diagonal = jnp.arange(ORDER)[:, None] == jnp.arange(ORDER)[None, :]
    real_gram = jnp.where(upper, square, square.T)
    imag_gram = jnp.where(upper, jnp.where(diagonal, 0.0, -square.T), square)
    return jnp.stack([real_gram, imag_gram], axis=0)


def per_device(series, starts, freqs, alpha):
    slab_cells = series.shape[1]
    n_space = lax.axis_size("space")
    n_freq = freqs.shape[0]
    n_out = n_freq // 2
    total_cells = slab_cells * n_space
    cells = slab_cells // n_out
    quarters = cells // LANES
    core = lax.rem(lax.axis_index("freq"), 2)
    same_core = [[2 * chip + side for chip in range(n_out)] for side in range(2)]

    mine = lax.all_to_all(
        split_cells(series, n_out), "freq", split_axis=0, concat_axis=0, tiled=True, axis_index_groups=same_core
    ).reshape(-1, cells)
    own_freqs = jnp.where(core == 0, freqs[0::2], freqs[1::2])
    table = transform_table(own_freqs, alpha).reshape(PARTS * SHIFTS * n_out, NFFT)
    scalars = jnp.concatenate([starts, core[None].astype(starts.dtype)])
    mine, table, scalars = lax.optimization_barrier((mine, table, scalars))
    other = lax.ppermute(mine, "freq", [(index, index ^ 1) for index in range(n_freq)])
    message = transform_and_gram(scalars, mine, other, table, n_out)
    received = lax.all_to_all(
        message, "freq", split_axis=0, concat_axis=0, tiled=True, axis_index_groups=same_core
    )
    own = received[:, : OWN * quarters].reshape(n_out, PARTS, NBLK, cells)
    spectra = jnp.transpose(own, (1, 2, 0, 3)).reshape(1, PARTS, NBLK, slab_cells)
    slab_gram = jnp.sum(received[:, OWN * quarters :].astype(jnp.float32), axis=0)
    spread = jnp.broadcast_to(slab_gram[None], (n_space, PAD // 2, LANES))
    slabs = lax.all_to_all(spread, "space", split_axis=0, concat_axis=0, tiled=True)
    gram = unpack_gram(jnp.sum(slabs, axis=0) / total_cells)[None]
    return (spectra, gram)


def solution(mesh):
    placed = (P("freq", "space"), P(), P(), P())
    return jax.shard_map(
        per_device,
        mesh=mesh,
        in_specs=placed,
        out_specs=(P("freq", None, None, "space"), P("freq", None, None, None)),
        check_vma=False,
    )
```
